256 devices in a mesh: row: 32 (over x, y, z_hi), rep: 8 (over z_lo, core).
Axes of the slice: x: 4, y: 4, z: 8 (z_hi: 2, z_lo: 4; z = z_hi * 4 + z_lo), core: 2. Of those that a mesh axis runs over, the one named last changes fastest.
Arguments:
- features: bfloat16 [65536, 256], P(('row', 'rep')), may hold values from -24 to 24
- weight: bfloat16 [256, 256], replicated, may hold values from -2 to 2
- degrees: int32 [65536], P(('row', 'rep')), may hold values from 1 to 16416, as said below
- cotangent: bfloat16 [65536, 256], P(('row', 'rep')), may hold values from -6 to 6
- tile_cols: int32 [4096, 16], P(('row', 'rep')), may hold values from 0 to 63, as said below
- list_len: int32 [4096], P(('row', 'rep')), may hold values from 1 to 16, as said below
- tiles: bfloat16 [4096, 16, 128, 128], P(('row', 'rep')), may hold values from 0 to 1, as said below
Outputs:
- activated: bfloat16 [65536, 256], P(('row', 'rep'))
- grad_x: bfloat16 [65536, 256], P(('row', 'rep'))
- grad_w: float32 [256, 256], P('row')
The draws below stay inside these ranges and needn't reach their ends.
Inputs may be any that keep to these rules, and one draw needn't show every extreme that they name: `tile_cols`: within one list the 16 column tiles are distinct. `list_len`: on every device some list has exactly 16 live slots. `tiles`: entries are 0 or 1. `degrees`: each node's degree exceeds the number of ones in its row of A; some node has exactly the largest value.
All inputs are finite; a program needn't handle non-finite values.
Results may differ from the reference program's by a relative error of at most 0.006.
Values may be sent and summed in bfloat16 or wider, within the bound.
No kernel may reach another device: no remote copies, remote signals or barrier semaphores. Data moves between devices by JAX's collectives and lax.ppermute only.
A program may use at most 128 MiB of HBM per device.

```python
import math
import jax
import jax.numpy as jnp
from jax import lax

F = 256
TILE = 128
KR = 16
SHARE = 256
BLOCK_ROWS = 2048
NODES = 65536
TROWS = 16
GCOLS = 64
LISTS = 4096
N_ROW = 32
N_REP = 8


def draw_tile_cols(key, part):
    key_list = jax.random.split(key, LISTS)

    def one_list(sub_key):
        return jax.random.permutation(sub_key, GCOLS)[:KR].astype(jnp.int32)
    return jax.vmap(one_list)(key_list)


def lengths_from(key):
    device_count = LISTS // TROWS
    own_key = jax.random.fold_in(key, 101)
    key_level, key_len, key_pick = jax.random.split(own_key, 3)
    load_level = jax.random.randint(key_level, (device_count, 1), 1, 5)
    most_len = jnp.maximum(load_level * KR // 4, 1)
    lengths = jax.random.randint(key_len, (device_count, TROWS), 1, most_len + 1)
    chosen = jax.random.randint(key_pick, (device_count, 1), 0, TROWS)
    positions = jnp.arange(TROWS)[None, :]
    lengths = jnp.where(positions == chosen, KR, lengths)
    return lengths.astype(jnp.int32)


def device_pattern(key, device_index):
    own_key = jax.random.fold_in(jax.random.fold_in(key, 202), device_index)
    key_density, key_bits = jax.random.split(own_key)
    density = jax.random.randint(key_density, (TROWS, KR, 1, 1), 15, 61)
    noise = jax.random.randint(key_bits, (TROWS, KR, TILE, TILE), 0, 1000)
    return jnp.where(noise < density, 1, 0).astype(jnp.int32)


def draw_list_len(key, part):
    return lengths_from(key).reshape(LISTS)


def draw_tiles(key, part):
    device_count = LISTS // TROWS

    def one_device(device_index):
        return device_pattern(key, device_index).astype(jnp.float32).astype(jnp.bfloat16)
    drawn = lax.map(one_device, jnp.arange(device_count))
    return drawn.reshape(LISTS, KR, TILE, TILE)


def draw_degrees(key, part):
    device_count = LISTS // TROWS
    lengths = lengths_from(key)

    def one_device(device_index):
        pattern = device_pattern(key, device_index)
        live = (jnp.arange(KR)[None, :] < lengths[device_index][:, None]).astype(jnp.int32)
        return jnp.sum(pattern.sum(axis=3) * live[:, :, None], axis=1)
    counts = lax.map(one_device, jnp.arange(device_count))
    counts = counts.reshape(N_ROW, N_REP, TROWS, TILE).sum(axis=1).reshape(NODES)
    extra = jax.random.randint(jax.random.fold_in(key, 303), (NODES,), 1, 33)
    top_degree = N_REP * KR * TILE + 32
    chosen = jax.random.randint(jax.random.fold_in(key, 404), (), 0, NODES)
    degrees = jnp.where(jnp.arange(NODES) == chosen, top_degree, counts + extra)
    return degrees.astype(jnp.int32)


def spiked(entries, key, source, target, parts, factor):
    owner, partner = [(jnp.arange(entries.shape[position]) // (entries.shape[position] // parts)).reshape([-1 if axis == position else 1 for axis in range(entries.ndim)]) for position in (source, target)]
    chosen = jax.random.permutation(key, parts)[partner]
    strong = (owner == chosen) | (owner == (partner + parts // 2) % parts)
    return jnp.where(strong, factor * entries, entries)


def level_of(key, extent, shards, least, high):
    level, own = 1.0, jax.random.fold_in(key, 6)
    for axis_at, parts in shards:
        heights = jnp.exp(jax.random.uniform(jax.random.fold_in(own, axis_at), (parts,), jnp.float32, least / len(shards), high / len(shards)))
        level = level * jnp.repeat(heights, extent[axis_at] // parts).reshape([-1 if axis == axis_at else 1 for axis in range(len(extent))])
    return level


def scatter_about(rng, shape, deviation, most, pieces=(), kind=jnp.bfloat16):
    array = deviation * jax.random.normal(rng, shape, jnp.float32)
    if pieces:
        array = array * level_of(rng, shape, pieces, -0.22, 0.18)
    return jnp.clip(array, -most, most).astype(kind)


def heavy_noise(key, extent, deviation, most, pieces, heavy, kind=jnp.bfloat16):
    values = deviation * jax.random.normal(key, extent, jnp.float32)
    if pieces:
        values = values * level_of(key, extent, pieces, -0.22, 0.18)
    return jnp.clip(spiked(values, jax.random.fold_in(key, 3), *heavy), -most, most).astype(kind)


def setup_inputs(seed: int = 0) -> dict:
    arg_keys = jax.random.split(jax.random.key(seed), 8)
    return {
        "features": heavy_noise(arg_keys[0], (NODES, F), 1.0, 24.0, ((0, 256),), (0, 1, 256, 6.0)),
        "weight": scatter_about(arg_keys[1], (F, F), (F // 32) ** -0.5, 2.0),
        "degrees": draw_degrees(jax.random.fold_in(arg_keys[7], 71), 0),
        "cotangent": scatter_about(arg_keys[3], (NODES, F), 1.0, 6.0, ((0, 256),)),
        "tile_cols": draw_tile_cols(jax.random.fold_in(arg_keys[7], 71), 0),
        "list_len": draw_list_len(jax.random.fold_in(arg_keys[7], 71), 0),
        "tiles": draw_tiles(jax.random.fold_in(arg_keys[7], 71), 0),
    }


def reference(features, weight, degrees, cotangent, tile_cols, list_len, tiles):
    width = features.shape[1]
    inv_root = 1.0 / jnp.sqrt(degrees.astype(jnp.float32))
    scaled = (features.astype(jnp.float32) * inv_root[:, None]).astype(jnp.bfloat16)
    section_view = scaled.reshape(N_ROW, N_REP, SHARE, width).transpose(1, 0, 2, 3).reshape(N_REP, GCOLS, TILE, width)
    slot_ids = jnp.arange(KR).astype(jnp.int32)
    live_slots = (slot_ids[None, :] < list_len[:, None]).astype(jnp.bfloat16)
    list_ids = jnp.arange(LISTS).astype(jnp.int32)

    def masked_tiles(list_index):
        return tiles[list_index] * live_slots[list_index][:, None, None]

    def forward_list(list_index):
        rep_group = list_index // TROWS % N_REP
        pattern = masked_tiles(list_index)
        row_tiles = pattern.transpose(1, 0, 2).reshape(TILE, KR * TILE)
        picked = section_view[rep_group][tile_cols[list_index]].reshape(KR * TILE, width)
        return jnp.dot(row_tiles, picked, preferred_element_type=jnp.float32)
    partial_value = lax.map(forward_list, list_ids)
    aggregate = partial_value.reshape(N_ROW, N_REP, BLOCK_ROWS, width).sum(axis=1).reshape(NODES, width)
    pooled = (aggregate * inv_root[:, None]).astype(jnp.bfloat16)
    preact = jnp.dot(pooled, weight, preferred_element_type=jnp.float32)
    activated = jax.nn.silu(preact).astype(jnp.bfloat16)
    sigmoid_val = jax.nn.sigmoid(preact)
    grad_pre = (cotangent.astype(jnp.float32) * sigmoid_val * (1.0 + preact * (1.0 - sigmoid_val))).astype(jnp.bfloat16)
    grad_w = lax.dot_general(pooled, grad_pre, (((0,), (0,)), ((), ())), preferred_element_type=jnp.float32) * (1.0 / math.sqrt(NODES))
    back_rows = (lax.dot_general(grad_pre, weight, (((1,), (1,)), ((), ())), preferred_element_type=jnp.float32) * inv_root[:, None]).astype(jnp.bfloat16)
    back_tiles = back_rows.reshape(N_ROW * TROWS, TILE, width)

    def backward_list(running, list_index):
        row_block = list_index // (N_REP * TROWS)
        rep_group = list_index // TROWS % N_REP
        tile_row = list_index % TROWS
        pattern = masked_tiles(list_index)
        col_tiles = pattern.transpose(0, 2, 1).reshape(KR * TILE, TILE)
        block_rows = back_tiles[row_block * TROWS + tile_row]
        contrib = jnp.dot(col_tiles, block_rows, preferred_element_type=jnp.float32).reshape(KR, TILE, width)
        running = running.at[rep_group, tile_cols[list_index]].add(contrib)
        return (running, None)
    zero_total = jnp.zeros((N_REP, GCOLS, TILE, width), jnp.float32)
    col_total, _ = lax.scan(backward_list, zero_total, list_ids)
    transposed = col_total.reshape(N_REP, N_ROW, SHARE, width).transpose(1, 0, 2, 3).reshape(NODES, width)
    grad_x = (transposed * inv_root[:, None]).astype(jnp.bfloat16)
    return (activated, grad_x, grad_w)
```

```python
import functools
import math

import jax
import jax.numpy as jnp
from jax import lax
from jax.experimental import pallas as pl
from jax.experimental.pallas import tpu as pltpu
from jax.sharding import PartitionSpec as P

BF16 = jnp.bfloat16
F32 = jnp.float32
SIDE, DEPTH = 4, 2
RUN, CORES = 4, 2
SHIFTS = (1, 3, 2)
TILE = 128
EXTRA = 8


def slot_of(shift):
    return shift + (shift == 2).astype(jnp.int32) - (shift == 3).astype(jnp.int32)


def row_shift(value, move):
    pairs = []
    for x in range(SIDE):
        for y in range(SIDE):
            for z in range(DEPTH):
                to_x, to_y, to_z = move(x, y, z)
                pairs.append(
                    ((x * SIDE + y) * DEPTH + z, (to_x * SIDE + to_y) * DEPTH + to_z)
                )
    return lax.ppermute(value, "row", pairs)


def shift_x(value, step):
    return row_shift(value, lambda x, y, z: ((x + step) % SIDE, y, z))


def shift_y(value, step):
    return row_shift(value, lambda x, y, z: (x, (y + step) % SIDE, z))


def flip_z(value):
    return row_shift(value, lambda x, y, z: (x, y, 1 - z))


def shift_run(value, step):
    pairs = [
        (run * CORES + core, (run + step) % RUN * CORES + core)
        for run in range(RUN)
        for core in range(CORES)
    ]
    return lax.ppermute(value, "rep", pairs)


def flip_core(value):
    pairs = [
        (run * CORES + core, run * CORES + 1 - core)
        for run in range(RUN)
        for core in range(CORES)
    ]
    return lax.ppermute(value, "rep", pairs)


def total(parts):
    return functools.reduce(jnp.add, [part.astype(F32) for part in parts])


def gather_rows(own):
    first, second = own, flip_z(own)
    firsts = [first] + [shift_x(first, step) for step in SHIFTS]
    seconds = [second] + [shift_y(second, step) for step in SHIFTS]
    first, second = jnp.concatenate(firsts), jnp.concatenate(seconds)
    firsts = [first] + [shift_y(first, step) for step in SHIFTS]
    seconds = [second] + [shift_x(second, step) for step in SHIFTS]
    return firsts + seconds


def forward_kernel(lists, cols, lens, tiles, *refs):
    pieces, (out, feats, sems) = refs[:-3], refs[-3:]
    step = pl.program_id(0)
    per_piece = feats.shape[0] // len(pieces)

    @pl.when(step == 0)
    def _():
        copies = [
            pltpu.make_async_copy(
                piece, feats.at[pl.ds(i * per_piece, per_piece)], sems.at[i]
            )
            for i, piece in enumerate(pieces)
        ]
        for copy in copies:
            copy.start()
        for copy in copies:
            copy.wait()

    row = lists[step]
    live = lens[row]
    slots = tiles.shape[1]
    half = slots // 2

    def part(first):
        left = [
            jnp.where(k < live, tiles[0, k], jnp.zeros_like(tiles[0, k]))
            for k in range(first, first + half)
        ]
        right = [feats[cols[row * slots + k]] for k in range(first, first + half)]
        return jnp.dot(
            jnp.concatenate(left, axis=1),
            jnp.concatenate(right, axis=0),
            preferred_element_type=F32,
        )

    @pl.when(live <= half)
    def _():
        out[0] = part(0).astype(out.dtype)

    @pl.when(live > half)
    def _():
        out[0] = (part(0) + part(half)).astype(out.dtype)


def forward(tiles, lists, cols, lens, pieces):
    count, slots, side, _ = tiles.shape
    width = pieces[0].shape[-1]
    pieces = [piece.reshape(-1, side, width) for piece in pieces]
    held = sum(piece.shape[0] for piece in pieces)
    return pl.pallas_call(
        forward_kernel,
        name="forward_product",
        out_shape=jax.ShapeDtypeStruct((lists.shape[0], side, width), BF16),
        grid_spec=pltpu.PrefetchScalarGridSpec(
            num_scalar_prefetch=3,
            grid=(lists.shape[0],),
            in_specs=[
                pl.BlockSpec((1, slots, side, side), lambda s, t, c, n: (t[s], 0, 0, 0))
            ]
            + [pl.BlockSpec(memory_space=pl.ANY)] * len(pieces),
            out_specs=pl.BlockSpec((1, side, width), lambda s, t, c, n: (s, 0, 0)),
            scratch_shapes=[
                pltpu.VMEM((held, side, width), BF16),
                pltpu.SemaphoreType.DMA((len(pieces),)),
            ],
        ),
        cost_estimate=pl.CostEstimate(
            flops=2 * lists.shape[0] * slots * side * side * width,
            bytes_accessed=2 * (lists.shape[0] * slots * side * side + held * side * width),
            transcendentals=0,
        ),
    )(lists, cols, lens, tiles, *pieces)


def middle_kernel(own, one, two, three, inv, cot, weight, act, back, grad):
    summed = (
        own[...].astype(F32)
        + one[...].astype(F32)
        + two[...].astype(F32)
        + three[...].astype(F32)
    )
    pooled = (summed * inv[...]).astype(BF16)
    pre = jnp.dot(pooled, weight[...], preferred_element_type=F32)
    sig = jax.nn.sigmoid(pre)
    act[...] = (pre * sig).astype(BF16)
    grad_pre = (cot[...].astype(F32) * sig * (1.0 + pre * (1.0 - sig))).astype(BF16)
    rows = lax.dot_general(
        grad_pre, weight[...], (((1,), (1,)), ((), ())), preferred_element_type=F32
    )
    back[...] = (rows * inv[...]).astype(BF16)
    grad[...] = lax.dot_general(
        pooled, grad_pre, (((0,), (0,)), ((), ())), preferred_element_type=F32
    )


def middle(parts, inv, cotangent, weight):
    rows, width = cotangent.shape
    return pl.pallas_call(
        middle_kernel,
        name="dense_middle",
        out_shape=(
            jax.ShapeDtypeStruct((rows, width), BF16),
            jax.ShapeDtypeStruct((rows, width), BF16),
            jax.ShapeDtypeStruct((width, width), F32),
        ),
    )(*parts, inv, cotangent, weight)


def backward_kernel(chunks, cols, lens, tiles, near, far, grad, out_a, out_b, sums, rows):
    step = pl.program_id(0)
    last = pl.num_programs(0) - 1
    half = pl.num_programs(0) // 2

    @pl.when(step == 0)
    def _():
        sums[...] = jnp.zeros_like(sums)

    @pl.when(step < half)
    def _():
        rows[...] = near[0]

    @pl.when(step >= half)
    def _():
        rows[...] = far[0]

    row = chunks[step]
    live = lens[row]
    slots = tiles.shape[1]
    group = 4
    for first in range(0, slots, group):

        @pl.when(first < live)
        def _():
            for k in range(first, first + group):
                tile = jnp.where(k < live, tiles[0, k], jnp.zeros_like(tiles[0, k]))
                place = cols[row * slots + k]
                sums[place] += lax.dot_general(
                    tile, rows[...], (((0,), (0,)), ((), ())), preferred_element_type=F32
                )

    @pl.when(step == last)
    def _():
        count = SIDE * SIDE * DEPTH
        base = pl.num_programs(0)

        @pl.loop(0, count)
        def _(i):
            out_a[i, pl.ds(0, TILE), :] = sums[i].astype(BF16)
            out_b[i] = sums[count + i].astype(BF16)
            source = pl.multiple_of(chunks[base + i] * EXTRA, EXTRA)
            out_a[i, pl.ds(TILE, EXTRA), :] = grad[pl.ds(source, EXTRA), :].astype(BF16)


def backward(tiles, table, cols, lens, near, far, grad):
    count, slots, side, _ = tiles.shape
    width = grad.shape[-1]
    near, far = [part.reshape(-1, side, width) for part in (near, far)]
    half = count // 2
    chunks = SIDE * SIDE * DEPTH
    whole = lambda *shape: pl.BlockSpec(shape, lambda s, t, c, n: (0,) * len(shape))
    return pl.pallas_call(
        backward_kernel,
        name="backward_product",
        out_shape=(
            jax.ShapeDtypeStruct((chunks, side + EXTRA, width), BF16),
            jax.ShapeDtypeStruct((chunks, side, width), BF16),
        ),
        grid_spec=pltpu.PrefetchScalarGridSpec(
            num_scalar_prefetch=3,
            grid=(count,),
            in_specs=[
                pl.BlockSpec((1, slots, side, side), lambda s, t, c, n: (t[s], 0, 0, 0)),
                pl.BlockSpec(
                    (1, side, width), lambda s, t, c, n: (jnp.minimum(s, half - 1), 0, 0)
                ),
                pl.BlockSpec(
                    (1, side, width), lambda s, t, c, n: (jnp.maximum(s - half, 0), 0, 0)
                ),
                whole(width, width),
            ],
            out_specs=(
                whole(chunks, side + EXTRA, width),
                whole(chunks, side, width),
            ),
            scratch_shapes=[
                pltpu.VMEM((2 * chunks, side, width), F32),
                pltpu.VMEM((side, width), BF16),
            ],
        ),
        cost_estimate=pl.CostEstimate(
            flops=2 * count * slots * side * side * width,
            bytes_accessed=2 * (count * slots * side * side + 4 * chunks * side * width),
            transcendentals=0,
        ),
    )(table, cols, lens, tiles, near, far, grad)


def scatter_rows(first, second):
    rows_a, rows_b, width = TILE + EXTRA, TILE, first.shape[-1]
    first = first.reshape(SIDE, SIDE * DEPTH * rows_a, width)
    second = second.reshape(SIDE, SIDE * DEPTH * rows_b, width)
    firsts = [first[0]] + [shift_x(first[step], step) for step in SHIFTS]
    seconds = [second[0]] + [shift_y(second[step], step) for step in SHIFTS]
    first = total(firsts).astype(BF16).reshape(SIDE, DEPTH * rows_a, width)
    second = total(seconds).astype(BF16).reshape(SIDE, DEPTH * rows_b, width)
    firsts = [first[0]] + [shift_y(first[step], step) for step in SHIFTS]
    seconds = [second[0]] + [shift_x(second[step], step) for step in SHIFTS]
    first, second = total(firsts), total(seconds)
    away = jnp.concatenate([first[rows_a:], second[rows_b:]]).astype(BF16)
    keep = jnp.concatenate([first[:rows_a], second[:rows_b]])
    return keep + flip_z(away).astype(F32)


def on_device(features, weight, degrees, cotangent, tile_cols, list_len, tiles):
    node_rows, width = features.shape
    count, slots = tile_cols.shape
    row_id, rep_id = lax.axis_index("row"), lax.axis_index("rep")
    x, y, z = row_id // (SIDE * DEPTH), row_id // DEPTH % SIDE, row_id % DEPTH
    run, core = rep_id // CORES, rep_id % CORES

    inv_root = 1.0 / jnp.sqrt(degrees.astype(F32))
    scaled = (features.astype(F32) * inv_root[:, None]).astype(BF16)
    inv_wide = jnp.broadcast_to(inv_root[:, None], (node_rows, width))

    share, part = tile_cols // 2, tile_cols % 2
    col_x, col_y, col_z = share // (SIDE * DEPTH), share // DEPTH % SIDE, share % DEPTH
    other = (col_z != z).astype(jnp.int32)
    from_x, from_y = slot_of((x - col_x) % SIDE), slot_of((y - col_y) % SIDE)
    near = jnp.where(other == 0, from_y * SIDE + from_x, from_x * SIDE + from_y)
    gather_cols = ((other * SIDE * SIDE + near) * 2 + part).reshape(-1)
    to_x, to_y = (col_x - x) % SIDE, (col_y - y) % SIDE
    far = jnp.where(part == 0, to_x * SIDE + to_y, to_y * SIDE + to_x)
    scatter_cols = ((part * SIDE * SIDE + far) * DEPTH + other).reshape(-1)

    order = jnp.arange(count)
    order_core = jnp.where(order < count // 2, core, 1 - core)
    steps = order // 2 % RUN
    sent_run, got_run = (run + steps) % RUN, (run - steps) % RUN
    sent_lists = (sent_run * CORES + order_core) * 2 + order % 2
    met = jnp.where(steps == 2, 3, jnp.where(steps == 3, 2, steps))
    met_run = (run - met) % RUN
    got_lists = (met_run * CORES + order_core) * 2 + order % 2
    chunk = jnp.arange(SIDE * SIDE * DEPTH)
    chunk_x, chunk_y = chunk // (SIDE * DEPTH), chunk // DEPTH % SIDE
    chunk_z = jnp.where(chunk % DEPTH == 0, z, 1 - z)
    chunk_rows = ((x + chunk_x) % SIDE * SIDE + (y + chunk_y) % SIDE) * DEPTH + chunk_z
    table = jnp.concatenate([got_lists, chunk_rows])

    pieces = gather_rows(scaled)
    partial_rows = forward(tiles, sent_lists, gather_cols, list_len, pieces)
    partial_rows = partial_rows.reshape(CORES, RUN, node_rows, width)
    mine = total([partial_rows[0], flip_core(partial_rows[1])]).astype(BF16)
    parts = [mine[0]] + [shift_run(mine[step], step) for step in SHIFTS]
    activated, back_rows, weight_part = middle(parts, inv_wide, cotangent, weight)

    near_rows = jnp.concatenate(
        [back_rows] + [shift_run(back_rows, step) for step in SHIFTS]
    )
    far_rows = flip_core(near_rows)
    first, second = backward(
        tiles, table, scatter_cols, list_len, near_rows, far_rows, weight_part
    )
    kept = scatter_rows(first, second)

    sums = jnp.concatenate([kept[:TILE], kept[TILE + EXTRA :]])
    grad_x = (sums * inv_root[:, None]).astype(BF16)
    weight_rows = kept[TILE : TILE + EXTRA]
    weight_rows = weight_rows + flip_core(weight_rows)
    weight_rows = total([weight_rows] + [shift_run(weight_rows, step) for step in SHIFTS])
    node_total = node_rows * lax.axis_size("row") * lax.axis_size("rep")
    return activated, grad_x, weight_rows * (1.0 / math.sqrt(node_total))


def solution(mesh):
    return jax.shard_map(
        on_device,
        mesh=mesh,
        in_specs=(
            P(("row", "rep"), None),
            P(),
            P(("row", "rep")),
            P(("row", "rep"), None),
            P(("row", "rep"), None),
            P(("row", "rep")),
            P(("row", "rep"), None, None, None),
        ),
        out_specs=(P(("row", "rep"), None), P(("row", "rep"), None), P("row", None)),
        check_vma=False,
    )
```

```python
import functools
import math

import jax
import jax.numpy as jnp
from jax import lax
from jax.experimental import pallas as pl
from jax.experimental.pallas import tpu as pltpu
from jax.sharding import PartitionSpec as P

BF16 = jnp.bfloat16
F32 = jnp.float32
SIDE, DEPTH = 4, 2
RUN, CORES = 4, 2
SHIFTS = (1, 3, 2)
TILE = 128
EXTRA = 8


def slot_of(shift):
    return shift + (shift == 2).astype(jnp.int32) - (shift == 3).astype(jnp.int32)


def row_shift(value, move):
    pairs = []
    for x in range(SIDE):
        for y in range(SIDE):
            for z in range(DEPTH):
                to_x, to_y, to_z = move(x, y, z)
                pairs.append(
                    ((x * SIDE + y) * DEPTH + z, (to_x * SIDE + to_y) * DEPTH + to_z)
                )
    return lax.ppermute(value, "row", pairs)


def shift_x(value, step):
    return row_shift(value, lambda x, y, z: ((x + step) % SIDE, y, z))


def shift_y(value, step):
    return row_shift(value, lambda x, y, z: (x, (y + step) % SIDE, z))


def flip_z(value):
    return row_shift(value, lambda x, y, z: (x, y, 1 - z))


def shift_run(value, step):
    pairs = [
        (run * CORES + core, (run + step) % RUN * CORES + core)
        for run in range(RUN)
        for core in range(CORES)
    ]
    return lax.ppermute(value, "rep", pairs)


def flip_core(value):
    pairs = [
        (run * CORES + core, run * CORES + 1 - core)
        for run in range(RUN)
        for core in range(CORES)
    ]
    return lax.ppermute(value, "rep", pairs)


def total(parts):
    return functools.reduce(jnp.add, [part.astype(F32) for part in parts])


def gather_rows(own):
    first, second = own, flip_z(own)
    firsts = [first] + [shift_x(first, step) for step in SHIFTS]
    seconds = [second] + [shift_y(second, step) for step in SHIFTS]
    first, second = lax.optimization_barrier(
        (jnp.concatenate(firsts), jnp.concatenate(seconds))
    )
    firsts = [first] + [shift_y(first, step) for step in SHIFTS]
    seconds = [second] + [shift_x(second, step) for step in SHIFTS]
    return firsts + seconds


def forward_kernel(lists, cols, lens, tiles, *refs):
    pieces, (out, feats, sems) = refs[:-3], refs[-3:]
    step = pl.program_id(0)
    per_piece = feats.shape[0] // len(pieces)

    @pl.when(step == 0)
    def _():
        copies = [
            pltpu.make_async_copy(
                piece, feats.at[pl.ds(i * per_piece, per_piece)], sems.at[i]
            )
            for i, piece in enumerate(pieces)
        ]
        for copy in copies:
            copy.start()
        for copy in copies:
            copy.wait()

    row = lists[step]
    live = lens[row]
    slots = tiles.shape[1]
    half = slots // 2

    def part(first):
        left = [
            jnp.where(k < live, tiles[0, k], jnp.zeros_like(tiles[0, k]))
            for k in range(first, first + half)
        ]
        right = [feats[cols[row * slots + k]] for k in range(first, first + half)]
        return jnp.dot(
            jnp.concatenate(left, axis=1),
            jnp.concatenate(right, axis=0),
            preferred_element_type=F32,
        )

    @pl.when(live <= half)
    def _():
        out[0] = part(0).astype(out.dtype)

    @pl.when(live > half)
    def _():
        out[0] = (part(0) + part(half)).astype(out.dtype)


def forward(tiles, lists, cols, lens, pieces):
    count, slots, side, _ = tiles.shape
    width = pieces[0].shape[-1]
    pieces = [piece.reshape(-1, side, width) for piece in pieces]
    held = sum(piece.shape[0] for piece in pieces)
    return pl.pallas_call(
        forward_kernel,
        name="forward_product",
        out_shape=jax.ShapeDtypeStruct((lists.shape[0], side, width), BF16),
        grid_spec=pltpu.PrefetchScalarGridSpec(
            num_scalar_prefetch=3,
            grid=(lists.shape[0],),
            in_specs=[
                pl.BlockSpec((1, slots, side, side), lambda s, t, c, n: (t[s], 0, 0, 0))
            ]
            + [pl.BlockSpec(memory_space=pl.ANY)] * len(pieces),
            out_specs=pl.BlockSpec((1, side, width), lambda s, t, c, n: (s, 0, 0)),
            scratch_shapes=[
                pltpu.VMEM((held, side, width), BF16),
                pltpu.SemaphoreType.DMA((len(pieces),)),
            ],
        ),
        cost_estimate=pl.CostEstimate(
            flops=2 * lists.shape[0] * slots * side * side * width,
            bytes_accessed=2 * (lists.shape[0] * slots * side * side + held * side * width),
            transcendentals=0,
        ),
    )(lists, cols, lens, tiles, *pieces)


def middle_kernel(own, one, two, three, inv, cot, weight, act, back, grad):
    summed = (
        own[...].astype(F32)
        + one[...].astype(F32)
        + two[...].astype(F32)
        + three[...].astype(F32)
    )
    pooled = (summed * inv[...]).astype(BF16)
    pre = jnp.dot(pooled, weight[...], preferred_element_type=F32)
    sig = jax.nn.sigmoid(pre)
    act[...] = (pre * sig).astype(BF16)
    grad_pre = (cot[...].astype(F32) * sig * (1.0 + pre * (1.0 - sig))).astype(BF16)
    rows = lax.dot_general(
        grad_pre, weight[...], (((1,), (1,)), ((), ())), preferred_element_type=F32
    )
    back[...] = (rows * inv[...]).astype(BF16)
    grad[...] = lax.dot_general(
        pooled, grad_pre, (((0,), (0,)), ((), ())), preferred_element_type=F32
    )


def middle(parts, inv, cotangent, weight):
    rows, width = cotangent.shape
    return pl.pallas_call(
        middle_kernel,
        name="dense_middle",
        out_shape=(
            jax.ShapeDtypeStruct((rows, width), BF16),
            jax.ShapeDtypeStruct((rows, width), BF16),
            jax.ShapeDtypeStruct((width, width), F32),
        ),
    )(*parts, inv, cotangent, weight)


def backward_kernel(chunks, cols, lens, tiles, near, far, grad, out_a, out_b, sums, rows):
    step = pl.program_id(0)
    last = pl.num_programs(0) - 1
    half = pl.num_programs(0) // 2

    @pl.when(step == 0)
    def _():
        sums[...] = jnp.zeros_like(sums)

    @pl.when(step < half)
    def _():
        rows[...] = near[0]

    @pl.when(step >= half)
    def _():
        rows[...] = far[0]

    row = chunks[step]
    live = lens[row]
    slots = tiles.shape[1]
    group = 4
    for first in range(0, slots, group):

        @pl.when(first < live)
        def _():
            for k in range(first, first + group):
                tile = jnp.where(k < live, tiles[0, k], jnp.zeros_like(tiles[0, k]))
                place = cols[row * slots + k]
                sums[place] += lax.dot_general(
                    tile, rows[...], (((0,), (0,)), ((), ())), preferred_element_type=F32
                )

    @pl.when(step == last)
    def _():
        count = SIDE * SIDE * DEPTH
        base = pl.num_programs(0)

        @pl.loop(0, count)
        def _(i):
            out_a[i, pl.ds(0, TILE), :] = sums[i].astype(BF16)
            out_b[i] = sums[count + i].astype(BF16)
            source = pl.multiple_of(chunks[base + i] * EXTRA, EXTRA)
            out_a[i, pl.ds(TILE, EXTRA), :] = grad[pl.ds(source, EXTRA), :].astype(BF16)


def backward(tiles, table, cols, lens, near, far, grad):
    count, slots, side, _ = tiles.shape
    width = grad.shape[-1]
    near, far = [part.reshape(-1, side, width) for part in (near, far)]
    half = count // 2
    chunks = SIDE * SIDE * DEPTH
    whole = lambda *shape: pl.BlockSpec(shape, lambda s, t, c, n: (0,) * len(shape))
    return pl.pallas_call(
        backward_kernel,
        name="backward_product",
        out_shape=(
            jax.ShapeDtypeStruct((chunks, side + EXTRA, width), BF16),
            jax.ShapeDtypeStruct((chunks, side, width), BF16),
        ),
        grid_spec=pltpu.PrefetchScalarGridSpec(
            num_scalar_prefetch=3,
            grid=(count,),
            in_specs=[
                pl.BlockSpec((1, slots, side, side), lambda s, t, c, n: (t[s], 0, 0, 0)),
                pl.BlockSpec(
                    (1, side, width), lambda s, t, c, n: (jnp.minimum(s, half - 1), 0, 0)
                ),
                pl.BlockSpec(
                    (1, side, width), lambda s, t, c, n: (jnp.maximum(s - half, 0), 0, 0)
                ),
                whole(width, width),
            ],
            out_specs=(
                whole(chunks, side + EXTRA, width),
                whole(chunks, side, width),
            ),
            scratch_shapes=[
                pltpu.VMEM((2 * chunks, side, width), F32),
                pltpu.VMEM((side, width), BF16),
            ],
        ),
        cost_estimate=pl.CostEstimate(
            flops=2 * count * slots * side * side * width,
            bytes_accessed=2 * (count * slots * side * side + 4 * chunks * side * width),
            transcendentals=0,
        ),
    )(table, cols, lens, tiles, near, far, grad)


def scatter_rows(first, second):
    rows_a, rows_b, width = TILE + EXTRA, TILE, first.shape[-1]
    first = first.reshape(SIDE, SIDE * DEPTH * rows_a, width)
    second = second.reshape(SIDE, SIDE * DEPTH * rows_b, width)
    firsts = [first[0]] + [shift_x(first[step], step) for step in SHIFTS]
    seconds = [second[0]] + [shift_y(second[step], step) for step in SHIFTS]
    first = total(firsts).astype(BF16).reshape(SIDE, DEPTH * rows_a, width)
    second = total(seconds).astype(BF16).reshape(SIDE, DEPTH * rows_b, width)
    firsts = [first[0]] + [shift_y(first[step], step) for step in SHIFTS]
    seconds = [second[0]] + [shift_x(second[step], step) for step in SHIFTS]
    first, second = total(firsts), total(seconds)
    away = jnp.concatenate([first[rows_a:], second[rows_b:]]).astype(BF16)
    keep = jnp.concatenate([first[:rows_a], second[:rows_b]])
    return keep + flip_z(away).astype(F32)


def on_device(features, weight, degrees, cotangent, tile_cols, list_len, tiles):
    node_rows, width = features.shape
    count, slots = tile_cols.shape
    row_id, rep_id = lax.axis_index("row"), lax.axis_index("rep")
    x, y, z = row_id // (SIDE * DEPTH), row_id // DEPTH % SIDE, row_id % DEPTH
    run, core = rep_id // CORES, rep_id % CORES

    inv_root = 1.0 / jnp.sqrt(degrees.astype(F32))
    scaled = (features.astype(F32) * inv_root[:, None]).astype(BF16)
    inv_wide = jnp.broadcast_to(inv_root[:, None], (node_rows, width))

    share, part = tile_cols // 2, tile_cols % 2
    col_x, col_y, col_z = share // (SIDE * DEPTH), share // DEPTH % SIDE, share % DEPTH
    other = (col_z != z).astype(jnp.int32)
    from_x, from_y = slot_of((x - col_x) % SIDE), slot_of((y - col_y) % SIDE)
    near = jnp.where(other == 0, from_y * SIDE + from_x, from_x * SIDE + from_y)
    gather_cols = ((other * SIDE * SIDE + near) * 2 + part).reshape(-1)
    to_x, to_y = (col_x - x) % SIDE, (col_y - y) % SIDE
    far = jnp.where(part == 0, to_x * SIDE + to_y, to_y * SIDE + to_x)
    scatter_cols = ((part * SIDE * SIDE + far) * DEPTH + other).reshape(-1)

    order = jnp.arange(count)
    order_core = jnp.where(order < count // 2, core, 1 - core)
    steps = order // 2 % RUN
    sent_run, got_run = (run + steps) % RUN, (run - steps) % RUN
    sent_lists = (sent_run * CORES + order_core) * 2 + order % 2
    met = jnp.where(steps == 2, 3, jnp.where(steps == 3, 2, steps))
    met_run = (run - met) % RUN
    got_lists = (met_run * CORES + order_core) * 2 + order % 2
    chunk = jnp.arange(SIDE * SIDE * DEPTH)
    chunk_x, chunk_y = chunk // (SIDE * DEPTH), chunk // DEPTH % SIDE
    chunk_z = jnp.where(chunk % DEPTH == 0, z, 1 - z)
    chunk_rows = ((x + chunk_x) % SIDE * SIDE + (y + chunk_y) % SIDE) * DEPTH + chunk_z
    table = jnp.concatenate([got_lists, chunk_rows])

    pieces = gather_rows(scaled)
    partial_rows = forward(tiles, sent_lists, gather_cols, list_len, pieces)
    partial_rows = partial_rows.reshape(CORES, RUN, node_rows, width)
    mine = total([partial_rows[0], flip_core(partial_rows[1])]).astype(BF16)
    parts = [mine[0]] + [shift_run(mine[step], step) for step in SHIFTS]
    activated, back_rows, weight_part = middle(parts, inv_wide, cotangent, weight)

    near_rows = jnp.concatenate(
        [back_rows] + [shift_run(back_rows, step) for step in SHIFTS]
    )
    far_rows = flip_core(near_rows)
    first, second = backward(
        tiles, table, scatter_cols, list_len, near_rows, far_rows, weight_part
    )
    kept = scatter_rows(first, second)

    sums = jnp.concatenate([kept[:TILE], kept[TILE + EXTRA :]])
    grad_x = (sums * inv_root[:, None]).astype(BF16)
    weight_rows = kept[TILE : TILE + EXTRA]
    weight_rows = weight_rows + flip_core(weight_rows)
    weight_rows = total([weight_rows] + [shift_run(weight_rows, step) for step in SHIFTS])
    node_total = node_rows * lax.axis_size("row") * lax.axis_size("rep")
    return activated, grad_x, weight_rows * (1.0 / math.sqrt(node_total))


def solution(mesh):
    return jax.shard_map(
        on_device,
        mesh=mesh,
        in_specs=(
            P(("row", "rep"), None),
            P(),
            P(("row", "rep")),
            P(("row", "rep"), None),
            P(("row", "rep"), None),
            P(("row", "rep")),
            P(("row", "rep"), None, None, None),
        ),
        out_specs=(P(("row", "rep"), None), P(("row", "rep"), None), P("row", None)),
        check_vma=False,
    )
```

```python
import functools
import math

import jax
import jax.numpy as jnp
from jax import lax
from jax.experimental import pallas as pl
from jax.experimental.pallas import tpu as pltpu
from jax.sharding import PartitionSpec as P

BF16 = jnp.bfloat16
F32 = jnp.float32
SIDE, DEPTH = 4, 2
RUN, CORES = 4, 2
SHIFTS = (1, 3, 2)
TILE = 128
EXTRA = 8


def slot_of(shift):
    return shift + (shift == 2).astype(jnp.int32) - (shift == 3).astype(jnp.int32)


def row_shift(value, move):
    pairs = []
    for x in range(SIDE):
        for y in range(SIDE):
            for z in range(DEPTH):
                to_x, to_y, to_z = move(x, y, z)
                pairs.append(
                    ((x * SIDE + y) * DEPTH + z, (to_x * SIDE + to_y) * DEPTH + to_z)
                )
    return lax.ppermute(value, "row", pairs)


def shift_x(value, step):
    return row_shift(value, lambda x, y, z: ((x + step) % SIDE, y, z))


def shift_y(value, step):
    return row_shift(value, lambda x, y, z: (x, (y + step) % SIDE, z))


def flip_z(value):
    return row_shift(value, lambda x, y, z: (x, y, 1 - z))


def shift_run(value, step):
    pairs = [
        (run * CORES + core, (run + step) % RUN * CORES + core)
        for run in range(RUN)
        for core in range(CORES)
    ]
    return lax.ppermute(value, "rep", pairs)


def flip_core(value):
    pairs = [
        (run * CORES + core, run * CORES + 1 - core)
        for run in range(RUN)
        for core in range(CORES)
    ]
    return lax.ppermute(value, "rep", pairs)


def total(parts):
    return functools.reduce(jnp.add, [part.astype(F32) for part in parts])


def gather_rows(own):
    first, second = own, flip_z(own)
    firsts = [first] + [shift_x(first, step) for step in SHIFTS]
    seconds = [second] + [shift_y(second, step) for step in SHIFTS]
    first, second = lax.optimization_barrier(
        (jnp.concatenate(firsts), jnp.concatenate(seconds))
    )
    firsts = [first] + [shift_y(first, step) for step in SHIFTS]
    seconds = [second] + [shift_x(second, step) for step in SHIFTS]
    return firsts + seconds


def forward_kernel(lists, cols, lens, tiles, *refs):
    pieces, (out, feats, sems) = refs[:-3], refs[-3:]
    step = pl.program_id(0)
    per_piece = feats.shape[0] // len(pieces)

    @pl.when(step == 0)
    def _():
        copies = [
            pltpu.make_async_copy(
                piece, feats.at[pl.ds(i * per_piece, per_piece)], sems.at[i]
            )
            for i, piece in enumerate(pieces)
        ]
        for copy in copies:
            copy.start()
        for copy in copies:
            copy.wait()

    row = lists[step]
    live = lens[row]
    slots = tiles.shape[1]
    half = slots // 2

    def part(first):
        left = [
            jnp.where(k < live, tiles[0, k], jnp.zeros_like(tiles[0, k]))
            for k in range(first, first + half)
        ]
        right = [feats[cols[row * slots + k]] for k in range(first, first + half)]
        return jnp.dot(
            jnp.concatenate(left, axis=1),
            jnp.concatenate(right, axis=0),
            preferred_element_type=F32,
        )

    @pl.when(live <= half)
    def _():
        out[0] = part(0).astype(out.dtype)

    @pl.when(live > half)
    def _():
        out[0] = (part(0) + part(half)).astype(out.dtype)


def forward(tiles, lists, cols, lens, pieces):
    count, slots, side, _ = tiles.shape
    width = pieces[0].shape[-1]
    pieces = [piece.reshape(-1, side, width) for piece in pieces]
    held = sum(piece.shape[0] for piece in pieces)
    return pl.pallas_call(
        forward_kernel,
        name="forward_product",
        out_shape=jax.ShapeDtypeStruct((lists.shape[0], side, width), BF16),
        grid_spec=pltpu.PrefetchScalarGridSpec(
            num_scalar_prefetch=3,
            grid=(lists.shape[0],),
            in_specs=[
                pl.BlockSpec((1, slots, side, side), lambda s, t, c, n: (t[s], 0, 0, 0))
            ]
            + [pl.BlockSpec(memory_space=pl.ANY)] * len(pieces),
            out_specs=pl.BlockSpec((1, side, width), lambda s, t, c, n: (s, 0, 0)),
            scratch_shapes=[
                pltpu.VMEM((held, side, width), BF16),
                pltpu.SemaphoreType.DMA((len(pieces),)),
            ],
        ),
        cost_estimate=pl.CostEstimate(
            flops=2 * lists.shape[0] * slots * side * side * width,
            bytes_accessed=2 * (lists.shape[0] * slots * side * side + held * side * width),
            transcendentals=0,
        ),
    )(lists, cols, lens, tiles, *pieces)


def middle_kernel(own, one, two, three, inv, cot, weight, act, back, grad):
    summed = (
        own[...].astype(F32)
        + one[...].astype(F32)
        + two[...].astype(F32)
        + three[...].astype(F32)
    )
    pooled = (summed * inv[...]).astype(BF16)
    pre = jnp.dot(pooled, weight[...], preferred_element_type=F32)
    sig = jax.nn.sigmoid(pre)
    act[...] = (pre * sig).astype(BF16)
    grad_pre = (cot[...].astype(F32) * sig * (1.0 + pre * (1.0 - sig))).astype(BF16)
    rows = lax.dot_general(
        grad_pre, weight[...], (((1,), (1,)), ((), ())), preferred_element_type=F32
    )
    back[...] = (rows * inv[...]).astype(BF16)
    grad[...] = lax.dot_general(
        pooled, grad_pre, (((0,), (0,)), ((), ())), preferred_element_type=F32
    )


def middle(parts, inv, cotangent, weight):
    rows, width = cotangent.shape
    return pl.pallas_call(
        middle_kernel,
        name="dense_middle",
        out_shape=(
            jax.ShapeDtypeStruct((rows, width), BF16),
            jax.ShapeDtypeStruct((rows, width), BF16),
            jax.ShapeDtypeStruct((width, width), F32),
        ),
    )(*parts, inv, cotangent, weight)


def backward_kernel(chunks, cols, lens, tiles, near, far, grad, out_a, out_b, sums, rows):
    step = pl.program_id(0)
    last = pl.num_programs(0) - 1
    half = pl.num_programs(0) // 2

    @pl.when(step == 0)
    def _():
        sums[...] = jnp.zeros_like(sums)

    @pl.when(step < half)
    def _():
        rows[...] = near[0]

    @pl.when(step >= half)
    def _():
        rows[...] = far[0]

    row = chunks[step]
    live = lens[row]
    slots = tiles.shape[1]
    group = 4
    for first in range(0, slots, group):

        @pl.when(first < live)
        def _():
            for k in range(first, first + group):
                tile = jnp.where(k < live, tiles[0, k], jnp.zeros_like(tiles[0, k]))
                place = cols[row * slots + k]
                sums[place] += lax.dot_general(
                    tile, rows[...], (((0,), (0,)), ((), ())), preferred_element_type=F32
                )

    @pl.when(step == last)
    def _():
        count = SIDE * SIDE * DEPTH
        base = pl.num_programs(0)

        @pl.loop(0, count)
        def _(i):
            out_a[i, pl.ds(0, TILE), :] = sums[i].astype(BF16)
            out_b[i] = sums[count + i].astype(BF16)
            source = pl.multiple_of(chunks[base + i] * EXTRA, EXTRA)
            out_a[i, pl.ds(TILE, EXTRA), :] = grad[pl.ds(source, EXTRA), :].astype(BF16)


def backward(tiles, table, cols, lens, near, far, grad):
    count, slots, side, _ = tiles.shape
    width = grad.shape[-1]
    near, far = [part.reshape(-1, side, width) for part in (near, far)]
    half = count // 2
    chunks = SIDE * SIDE * DEPTH
    whole = lambda *shape: pl.BlockSpec(shape, lambda s, t, c, n: (0,) * len(shape))
    return pl.pallas_call(
        backward_kernel,
        name="backward_product",
        out_shape=(
            jax.ShapeDtypeStruct((chunks, side + EXTRA, width), BF16),
            jax.ShapeDtypeStruct((chunks, side, width), BF16),
        ),
        grid_spec=pltpu.PrefetchScalarGridSpec(
            num_scalar_prefetch=3,
            grid=(count,),
            in_specs=[
                pl.BlockSpec((1, slots, side, side), lambda s, t, c, n: (t[s], 0, 0, 0)),
                pl.BlockSpec(
                    (1, side, width), lambda s, t, c, n: (jnp.minimum(s, half - 1), 0, 0)
                ),
                pl.BlockSpec(
                    (1, side, width), lambda s, t, c, n: (jnp.maximum(s - half, 0), 0, 0)
                ),
                whole(width, width),
            ],
            out_specs=(
                whole(chunks, side + EXTRA, width),
                whole(chunks, side, width),
            ),
            scratch_shapes=[
                pltpu.VMEM((2 * chunks, side, width), F32),
                pltpu.VMEM((side, width), BF16),
            ],
        ),
        cost_estimate=pl.CostEstimate(
            flops=2 * count * slots * side * side * width,
            bytes_accessed=2 * (count * slots * side * side + 4 * chunks * side * width),
            transcendentals=0,
        ),
    )(table, cols, lens, tiles, near, far, grad)


def scatter_rows(first, second):
    rows_a, rows_b, width = TILE + EXTRA, TILE, first.shape[-1]
    first = first.reshape(SIDE, SIDE * DEPTH * rows_a, width)
    second = second.reshape(SIDE, SIDE * DEPTH * rows_b, width)
    firsts = [first[0]] + [shift_x(first[step], step) for step in SHIFTS]
    seconds = [second[0]] + [shift_y(second[step], step) for step in SHIFTS]
    first = total(firsts).astype(BF16).reshape(SIDE, DEPTH * rows_a, width)
    second = total(seconds).astype(BF16).reshape(SIDE, DEPTH * rows_b, width)
    firsts = [first[0]] + [shift_y(first[step], step) for step in SHIFTS]
    seconds = [second[0]] + [shift_x(second[step], step) for step in SHIFTS]
    first, second = total(firsts), total(seconds)
    away_grad = first[rows_a + TILE :].astype(BF16)
    grad = first[TILE:rows_a] + flip_z(away_grad).astype(F32)
    away = jnp.concatenate(
        [first[rows_a : rows_a + TILE], second[rows_b:]]
    ).astype(BF16)
    keep = jnp.concatenate([first[:TILE], second[:rows_b]])
    return keep + flip_z(away).astype(F32), grad


def on_device(features, weight, degrees, cotangent, tile_cols, list_len, tiles):
    node_rows, width = features.shape
    count, slots = tile_cols.shape
    row_id, rep_id = lax.axis_index("row"), lax.axis_index("rep")
    x, y, z = row_id // (SIDE * DEPTH), row_id // DEPTH % SIDE, row_id % DEPTH
    run, core = rep_id // CORES, rep_id % CORES

    inv_root = 1.0 / jnp.sqrt(degrees.astype(F32))
    scaled = (features.astype(F32) * inv_root[:, None]).astype(BF16)
    inv_wide = jnp.broadcast_to(inv_root[:, None], (node_rows, width))

    share, part = tile_cols // 2, tile_cols % 2
    col_x, col_y, col_z = share // (SIDE * DEPTH), share // DEPTH % SIDE, share % DEPTH
    other = (col_z != z).astype(jnp.int32)
    from_x, from_y = slot_of((x - col_x) % SIDE), slot_of((y - col_y) % SIDE)
    near = jnp.where(other == 0, from_y * SIDE + from_x, from_x * SIDE + from_y)
    gather_cols = ((other * SIDE * SIDE + near) * 2 + part).reshape(-1)
    to_x, to_y = (col_x - x) % SIDE, (col_y - y) % SIDE
    far = jnp.where(part == 0, to_x * SIDE + to_y, to_y * SIDE + to_x)
    scatter_cols = ((part * SIDE * SIDE + far) * DEPTH + other).reshape(-1)

    order = jnp.arange(count)
    order_core = jnp.where(order < count // 2, core, 1 - core)
    steps = order // 2 % RUN
    sent_run, got_run = (run + steps) % RUN, (run - steps) % RUN
    sent_lists = (sent_run * CORES + order_core) * 2 + order % 2
    met = jnp.where(steps == 2, 3, jnp.where(steps == 3, 2, steps))
    met_run = (run - met) % RUN
    got_lists = (met_run * CORES + order_core) * 2 + order % 2
    chunk = jnp.arange(SIDE * SIDE * DEPTH)
    chunk_x, chunk_y = chunk // (SIDE * DEPTH), chunk // DEPTH % SIDE
    chunk_z = jnp.where(chunk % DEPTH == 0, z, 1 - z)
    chunk_rows = ((x + chunk_x) % SIDE * SIDE + (y + chunk_y) % SIDE) * DEPTH + chunk_z
    table = jnp.concatenate([got_lists, chunk_rows])

    pieces = gather_rows(scaled)
    partial_rows = forward(tiles, sent_lists, gather_cols, list_len, pieces)
    partial_rows = partial_rows.reshape(CORES, RUN, node_rows, width)
    mine = total([partial_rows[0], flip_core(partial_rows[1])]).astype(BF16)
    parts = [mine[0]] + [shift_run(mine[step], step) for step in SHIFTS]
    activated, back_rows, weight_part = middle(parts, inv_wide, cotangent, weight)

    near_rows = jnp.concatenate(
        [back_rows] + [shift_run(back_rows, step) for step in SHIFTS]
    )
    far_rows = flip_core(near_rows)
    first, second = backward(
        tiles, table, scatter_cols, list_len, near_rows, far_rows, weight_part
    )
    sums, weight_rows = scatter_rows(first, second)

    grad_x = (sums * inv_root[:, None]).astype(BF16)
    weight_rows = weight_rows + flip_core(weight_rows)
    weight_rows = total([weight_rows] + [shift_run(weight_rows, step) for step in SHIFTS])
    node_total = node_rows * lax.axis_size("row") * lax.axis_size("rep")
    return activated, grad_x, weight_rows * (1.0 / math.sqrt(node_total))


def solution(mesh):
    return jax.shard_map(
        on_device,
        mesh=mesh,
        in_specs=(
            P(("row", "rep"), None),
            P(),
            P(("row", "rep")),
            P(("row", "rep"), None),
            P(("row", "rep"), None),
            P(("row", "rep")),
            P(("row", "rep"), None, None, None),
        ),
        out_specs=(P(("row", "rep"), None), P(("row", "rep"), None), P("row", None)),
        check_vma=False,
    )
```
